32 devices in a mesh: dp: 16 (over z, y, core), owner: 2 (over x).
Axes of the slice: x: 2, y: 2, z: 4, core: 2. Of those that a mesh axis runs over, the one named last changes fastest.
Arguments:
- hidden: bfloat16 [2048, 4096], P('dp'), may hold values from -6 to 6
- norm_gain: float32 [4096], replicated, may hold values from 0.3 to 3
- cotangent: bfloat16 [2048, 6144], P('dp'), may hold values from -30 to 30
Outputs:
- update: bfloat16 [6144, 4096], P('dp', 'owner')
The draws below stay inside these ranges and needn't reach their ends.
All inputs are finite; a program needn't handle non-finite values. Where the reference program divides by a largest or mean magnitude, that divisor is 1e-20 or more.
Results may differ from the reference program's by a relative error of at most 0.014.
Values may be sent and summed in bfloat16 or wider, within the bound.
A program may use at most 128 MiB of HBM per device.

```python
import math
import jax
import jax.numpy as jnp
from jax import lax

D = 4096
TILE = 1024
TOK_DEV = 128
TOKENS = 2048
DOUT = 6144
NBLK = 10
N_DP = 16


latent_rank = 16


def shared_latent(key):
    return jax.random.normal(jax.random.fold_in(key, 5), (TOKENS, latent_rank), jnp.float32)


def draw_hidden(key, part):
    latent = shared_latent(key)
    keys = jax.random.split(jax.random.fold_in(key, 23), 2)
    basis = jax.random.normal(keys[0], (latent_rank, D), jnp.float32) / math.sqrt(latent_rank)
    noise = jax.random.normal(keys[1], (TOKENS, D), jnp.float32)
    share = 0.5
    mixed = jnp.dot(latent, basis)
    values = math.sqrt(1.0 - share * share) * noise + share * mixed
    return jnp.clip(values, -6.0, 6.0).astype(jnp.bfloat16)


def draw_cotangent(key, part):
    latent = shared_latent(key)
    keys = jax.random.split(jax.random.fold_in(key, 17), 8)
    columns = 3.0 ** (jnp.arange(DOUT, dtype=jnp.float32) / DOUT)
    columns = columns * jax.random.uniform(keys[1], (DOUT,), jnp.float32, 0.5, 1.5)
    heavy = jax.random.randint(keys[4], (), 0, N_DP)
    group_index = jnp.arange(TOKENS, dtype=jnp.int32) // TOK_DEV
    before = (heavy + N_DP - 1) % N_DP
    chosen = jnp.logical_or(group_index == heavy, group_index == before)
    group_scale = jnp.where(chosen, 5.0, 1.0).astype(jnp.float32)[:, None]
    common_basis = jax.random.normal(keys[5], (latent_rank, DOUT), jnp.float32) / math.sqrt(latent_rank)
    own_basis = jax.random.normal(keys[6], (N_DP, latent_rank, DOUT), jnp.float32) / math.sqrt(latent_rank)
    own_latent = jax.random.normal(keys[7], (N_DP, TOK_DEV, latent_rank), jnp.float32)
    own = jnp.einsum('gtr,grc->gtc', own_latent, own_basis).reshape(TOKENS, DOUT)
    common = jnp.dot(latent, common_basis)
    noise = jax.random.normal(keys[0], (TOKENS, DOUT), jnp.float32)
    noise_share = 0.6
    common_share = 0.4
    own_share = math.sqrt(1.0 - noise_share * noise_share - common_share * common_share)
    values = noise_share * noise + common_share * common + own_share * own
    values = values * group_scale
    return jnp.clip(values * columns, -30.0, 30.0).astype(jnp.bfloat16)


def setup_inputs(seed: int = 0) -> dict:
    arg_keys = jax.random.split(jax.random.key(seed), 4)
    hidden = draw_hidden(jax.random.fold_in(arg_keys[3], 71), 0)
    norm_gain = jnp.clip(jnp.exp(jax.random.uniform(arg_keys[1], (D,), jnp.float32, math.log(0.3), math.log(3.0))), 0.3, 3.0)
    cotangent = draw_cotangent(jax.random.fold_in(arg_keys[3], 71), 0)
    return {"hidden": hidden, "norm_gain": norm_gain, "cotangent": cotangent}


DAMPING = 0.1

def rounded(value):
    return lax.optimization_barrier(value.astype(jnp.bfloat16)).astype(jnp.float32)

def reference(hidden, norm_gain, cotangent):
    highest = lax.Precision.HIGHEST
    states = hidden.astype(jnp.float32)
    normed = (states * lax.rsqrt(lax.optimization_barrier(jnp.mean(states * states, axis=1, keepdims=True)) + 1e-05) * norm_gain).astype(jnp.bfloat16)
    source = jnp.concatenate([normed, cotangent], axis=1)
    identity = jnp.eye(TILE, dtype=jnp.float32)
    results = []
    for block in range(NBLK):
        piece = source[:, block * TILE:(block + 1) * TILE].astype(jnp.float32)
        factor = jnp.dot(piece.T, piece, precision=highest)
        matrix = factor / TOKENS + DAMPING * identity
        scale = 1.0 / jnp.max(lax.optimization_barrier(jnp.sum(jnp.abs(matrix), axis=1)))
        first = 2.0 * scale * identity - scale * scale * matrix
        first_low = rounded(first)
        product = rounded(jnp.dot(first_low, rounded(matrix), precision=highest))
        inverse = rounded(2.0 * first - jnp.dot(product, first_low, precision=highest))
        results.append(jnp.dot(piece, inverse, precision=highest).astype(jnp.bfloat16))
    inputs_side = D // TILE
    pre_in = jnp.concatenate(results[:inputs_side], axis=1).astype(jnp.float32).reshape(N_DP, TOK_DEV, D)
    pre_out = jnp.concatenate(results[inputs_side:], axis=1).astype(jnp.float32).reshape(N_DP, TOK_DEV, DOUT)

    def accumulate(total, pair):
        left, right = pair
        return (total + rounded(jnp.dot(right.T, left, precision=highest)), None)
    summed, _ = lax.scan(accumulate, jnp.zeros((DOUT, D), jnp.float32), (pre_in, pre_out))
    squares = jnp.sum(summed * summed)
    return (summed * lax.rsqrt(squares / (D * DOUT) + 1e-06)).astype(jnp.bfloat16)
```

```python
import jax
import jax.numpy as jnp
from jax import lax
from jax.sharding import PartitionSpec as P

TILE = 1024


DAMPING = 0.1


def contract(left, right, left_dim, right_dim):
    return lax.dot_general(
        left, right, (((left_dim,), (right_dim,)), ((), ())), preferred_element_type=jnp.float32
    )


def inverse_of(piece, tokens):
    identity = jnp.eye(TILE, dtype=jnp.float32)
    matrix = contract(piece, piece, 0, 0) / tokens + DAMPING * identity
    scale = 1.0 / jnp.max(jnp.sum(jnp.abs(matrix), axis=1))
    first = 2.0 * scale * identity - (scale * scale) * matrix
    first_low = first.astype(jnp.bfloat16)
    matrix_low = matrix.astype(jnp.bfloat16)
    product = contract(first_low, matrix_low, 1, 0).astype(jnp.bfloat16)
    return (2.0 * first - contract(product, first_low, 1, 0)).astype(jnp.bfloat16)


def shards(hidden, norm_gain, cotangent):
    owners = lax.axis_size("owner")
    position = lax.axis_index("owner")
    groups = lax.axis_size("dp")
    group = lax.axis_index("dp")
    tokens_here = hidden.shape[0]
    tokens = tokens_here * groups
    width = hidden.shape[1]
    out_width = cotangent.shape[1]
    strip = out_width // groups
    own = width // owners
    in_width = max(own, TILE)

    firsts = jnp.array([(g * strip) // TILE for g in range(groups)], jnp.int32)
    lasts = jnp.array([((g + 1) * strip - 1) // TILE for g in range(groups)], jnp.int32)
    odd = lax.rem(position, 2) == 1
    wanted = jnp.where(odd, lasts, firsts)
    outgoing = jnp.stack(
        [
            lax.dynamic_slice_in_dim(cotangent, wanted[g] * TILE, TILE, 1)
            for g in range(groups)
        ]
    )
    out_piece = lax.all_to_all(outgoing, "dp", 0, 0, tiled=True).reshape(tokens, TILE)

    states = hidden.astype(jnp.float32)
    normed = (
        states * lax.rsqrt(jnp.mean(states * states, axis=1, keepdims=True) + 1e-05) * norm_gain
    ).astype(jnp.bfloat16)
    in_start = (position * own) // TILE * TILE
    mine = lax.dynamic_slice_in_dim(normed, in_start, in_width, 1)
    in_piece = lax.all_gather(mine, "dp", axis=0, tiled=True)

    out_inverse = inverse_of(out_piece, tokens)
    padded = jnp.pad(out_inverse, ((0, 0), (strip, strip)))
    offset = group * strip - wanted[group] * TILE
    strip_inverse = lax.dynamic_slice_in_dim(padded, offset + strip, strip, 1)
    part = contract(out_piece, strip_inverse, 1, 0).astype(jnp.bfloat16)
    other = lax.ppermute(part, "owner", [(o, o ^ 1) for o in range(owners)])
    column_block = (group * strip + jnp.arange(strip, dtype=jnp.int32)) // TILE
    pre_out = jnp.where((column_block == wanted[group])[None, :], part, other)

    results = []
    for block in range(in_width // TILE):
        piece = in_piece[:, block * TILE : (block + 1) * TILE]
        inverse = inverse_of(piece, tokens)
        if own < TILE:
            inverse = lax.dynamic_slice_in_dim(inverse, position * own - in_start, own, 1)
        cross = contract(pre_out, piece, 0, 0).astype(jnp.bfloat16)
        results.append(contract(cross, inverse, 1, 0))
    summed = jnp.concatenate(results, axis=1)
    squares = lax.psum(jnp.sum(summed * summed), ("dp", "owner"))
    return (summed * lax.rsqrt(squares / (width * out_width) + 1e-06)).astype(jnp.bfloat16)


def solution(mesh):
    in_specs = (P("dp", None), P(), P("dp", None))
    out_specs = P("dp", "owner")
    return jax.shard_map(shards, mesh=mesh, in_specs=in_specs, out_specs=out_specs, check_vma=False)
```
